32 devices in a mesh: groups: 2 (over x), tm: 16 (over z, y, core).
Axes of the slice: x: 2, y: 2, z: 4, core: 2. Of those that a mesh axis runs over, the one named last changes fastest.
Arguments:
- latents: bfloat16 [128, 128, 256], P(('groups', 'tm')), parts along dimension 0, may hold values from -6 to 6
- clip_lengths: int32 [8], P('groups'), parts along dimension 0, may hold values from 1 to 48, 64 in all
- norm1_gain: float32 [256], replicated, may hold values from 0.1 to 1.9
- conv1_weight: bfloat16 [6912, 256], replicated, may hold values from -0.078125 to 0.078125
- norm2_gain: float32 [256], replicated, may hold values from 0.1 to 1.9
- conv2_weight: bfloat16 [6912, 256], replicated, may hold values from -0.078125 to 0.078125
- norm3_gain: float32 [256], replicated, may hold values from 0.1 to 1.9
- query_weight: bfloat16 [256, 512], replicated, may hold values from -4 to 4, as said below
- key_weight: bfloat16 [256, 512], replicated, may hold values from -4 to 4, as said below
- value_weight: bfloat16 [256, 512], replicated, may hold values from -0.375 to 0.375
- out_weight: bfloat16 [512, 256], replicated, may hold values from -0.25 to 0.25
Outputs:
- encoded: bfloat16 [128, 128, 256], P(('groups', 'tm')), parts along dimension 0
The draws below stay inside these ranges and needn't reach their ends.
There are 2 independent parts, one for each index of `groups`. The reference program is written for one: setup_inputs(seed, part) draws one part's arguments, and reference() takes and returns one part's arrays. A program takes and returns all parts, laid end to end along the dimension named above; an argument that names none is the same for every part. Nothing has to cross between parts.
Inputs may be any that keep to these rules, and one draw needn't show every extreme that they name: `clip_lengths`: packing order of the clips; at least one clip has exactly 48 frames and all lengths sum to 64. `query_weight`: a projection matrix. `key_weight`: a projection matrix.
All inputs are finite; a program needn't handle non-finite values.
Results may differ from the reference program's by a relative error of at most 0.035.
Values may be sent and summed in bfloat16 or wider, within the bound.
A program may use at most 256 MiB of HBM per device.

```python
import math
import jax
import jax.numpy as jnp
import numpy as np
from jax import lax

C = 256
HEADS = 8
HEAD_DIM = 64
INNER = 512
NORM_GROUPS = 32
HT = 8
WT = 16
S = 128
REACH = 12
CLIP_MAX = 48
NFRAMES = 64
NCLIPS = 4
N_TM = 16


def apart_projection(key, salt_base, salt_gain):
    base = jax.random.truncated_normal(jax.random.fold_in(key, salt_base), -2.5, 2.5, (C, INNER), jnp.float32) * C ** (-0.5)
    head_gain = jnp.exp(jax.random.uniform(jax.random.fold_in(key, salt_gain), (HEADS,), jnp.float32, math.log(2.0), math.log(4.0)))
    return base * jnp.repeat(head_gain, HEAD_DIM)[None, :]


def draw_query_weight(key, part):
    return apart_projection(key, 1, 5).astype(jnp.bfloat16)


def draw_key_weight(key, part):
    return apart_projection(key, 2, 7).astype(jnp.bfloat16)


def shard_levels(key, extent, cuts, low, top_value):
    factor_of = 1.0
    for axis_at, blocks in cuts:
        draws = jax.random.uniform(jax.random.fold_in(jax.random.fold_in(key, 6), axis_at), (blocks,), jnp.float32, low / len(cuts), top_value / len(cuts))
        factor_of = factor_of * jnp.repeat(jnp.exp(draws), extent[axis_at] // blocks).reshape((-1,) + (1,) * (len(extent) - 1 - axis_at))
    return factor_of


def length_profile(number_of, total, reach, skew):
    loads = [(1 << 20) // math.isqrt(standing ** skew) + 1 for standing in range(2, number_of + 1)]
    spare, counts = total - reach - (number_of - 1), [1] * (number_of - 1)
    while spare > 0:
        candidates = [i for i in range(number_of - 1) if counts[i] < reach]
        whole, budget = sum([loads[i] for i in candidates]), spare
        for i in candidates:
            addition = min(reach - counts[i], max(1, budget * loads[i] // whole), spare)
            counts[i] = counts[i] + addition
            spare = spare - addition
    return np.array([reach] + counts)


def ragged(rng, amount, total, bound, skew):
    if amount == 2:
        one = jax.random.randint(rng, (), max(1, total - bound), min(bound, total - 1) + 1)
        return jnp.stack([one, total - one])
    tallies = jnp.asarray(length_profile(amount, total, bound, skew), jnp.int32)
    pairs = (amount - 1) // 2
    source_of, receiver = tallies[1:1 + 2 * pairs:2], tallies[2:2 + 2 * pairs:2]
    room = jnp.minimum(source_of - 1, bound - receiver)
    moved = jax.random.randint(jax.random.fold_in(rng, 1), (pairs,), 0, 1 << 20) % (room + 1)
    tallies = tallies.at[1:1 + 2 * pairs:2].set(source_of - moved).at[2:2 + 2 * pairs:2].set(receiver + moved)
    return tallies[jax.random.permutation(jax.random.fold_in(rng, 2), amount)]


def centred(rng, shape, deviation, reach, cuts=(), held_as=jnp.bfloat16):
    level = shard_levels(rng, shape, cuts, -0.22, 0.18) if cuts else 1.0
    values = jax.random.normal(rng, shape, jnp.float32) * deviation * level
    return jnp.minimum(jnp.maximum(values, -reach), reach).astype(held_as)


def setup_inputs(seed: int = 0, part: int = 0) -> dict:
    seeds = jax.random.split(jax.random.key(seed), 12)
    part_splits = jax.random.split(jax.random.fold_in(seeds[11], part), 12)
    return {
        "latents": centred(part_splits[0], (NFRAMES, S, C), 1.0, 6.0, ((0, 16),)),
        "clip_lengths": ragged(part_splits[1], NCLIPS, NFRAMES, CLIP_MAX, 2).astype(jnp.int32),
        "norm1_gain": jnp.clip(1.0 + 0.18 * jax.random.normal(seeds[2], (C,), jnp.float32), 0.1, 1.9),
        "conv1_weight": centred(seeds[3], (27 * C, C), (27 * C) ** -0.5, 0.078125),
        "norm2_gain": jnp.clip(1.0 + 0.18 * jax.random.normal(seeds[4], (C,), jnp.float32), 0.1, 1.9),
        "conv2_weight": centred(seeds[5], (27 * C, C), (27 * C) ** -0.5, 0.078125),
        "norm3_gain": jnp.clip(1.0 + 0.18 * jax.random.normal(seeds[6], (C,), jnp.float32), 0.1, 1.9),
        "query_weight": draw_query_weight(jax.random.fold_in(seeds[11], 71), part),
        "key_weight": draw_key_weight(jax.random.fold_in(seeds[11], 71), part),
        "value_weight": centred(seeds[9], (C, INNER), C ** -0.5, 0.375),
        "out_weight": centred(seeds[10], (INNER, C), INNER ** -0.5, 0.25),
    }


def clip_index(positions, clip_lengths):
    finish = jnp.cumsum(clip_lengths).astype(jnp.int32)
    return lax.optimization_barrier(jnp.sum((positions[:, None] >= finish[None, :]).astype(jnp.int32), axis=1))

def packed_place(frame_ids, clip_lengths, total):
    finish = jnp.cumsum(clip_lengths).astype(jnp.int32)
    starts = finish - clip_lengths.astype(jnp.int32)
    longest = jnp.argmax(clip_lengths).astype(jnp.int32)
    first = starts[longest]
    offset = jnp.mod(total - CLIP_MAX // 2 - first, total).astype(jnp.int32)
    positions = jnp.mod(frame_ids - offset, total).astype(jnp.int32)
    return (positions, clip_index(positions, clip_lengths))

def group_norm(values, gain):
    frames, cells, width = values.shape
    split = values.reshape(frames, cells, NORM_GROUPS, width // NORM_GROUPS)
    center = lax.optimization_barrier(jnp.mean(split, axis=(1, 3), keepdims=True))
    spread = lax.optimization_barrier(jnp.mean(jnp.square(split - center), axis=(1, 3), keepdims=True))
    normal_part = (split - center) * lax.rsqrt(spread + 1e-06)
    return normal_part.reshape(frames, cells, width) * gain

def tap_columns(padded):
    pieces = []
    for step in range(3):
        for row in range(3):
            for col in range(3):
                pieces.append(padded[:, step, row:row + HT, col:col + WT, :])
    joined = jnp.concatenate(pieces, axis=-1)
    return joined.reshape(-1, joined.shape[-1])

def causal_conv(inputs, weight, keep_one, keep_two):
    nframes, cells, width = inputs.shape
    extended = jnp.concatenate([inputs[nframes - 2:], inputs], axis=0)
    back_two = extended[:nframes] * keep_two[:, None, None]
    back_one = extended[1:nframes + 1] * keep_one[:, None, None]
    stacked = jnp.stack([back_two, back_one, inputs], axis=1).reshape(nframes, 3, HT, WT, width)
    padded = jnp.pad(stacked, ((0, 0), (0, 0), (1, 1), (1, 1), (0, 0)))
    blocks = padded.reshape(N_TM, nframes // N_TM, 3, HT + 2, WT + 2, width)

    def one_block(block):
        return jnp.dot(tap_columns(block), weight, preferred_element_type=jnp.float32)
    return lax.map(one_block, blocks).reshape(nframes, cells, width)

def reference(latents, clip_lengths, norm1_gain, conv1_weight, norm2_gain, conv2_weight, norm3_gain, query_weight, key_weight, value_weight, out_weight):
    nframes, cells, width = latents.shape
    frame_ids = jnp.arange(nframes, dtype=jnp.int32)
    own_pos, own_clip = packed_place(frame_ids, clip_lengths, nframes)
    prev_one = packed_place(jnp.mod(frame_ids - 1, nframes).astype(jnp.int32), clip_lengths, nframes)[1]
    prev_two = packed_place(jnp.mod(frame_ids - 2, nframes).astype(jnp.int32), clip_lengths, nframes)[1]
    keep_one = ((own_pos >= 1) & (prev_one == own_clip)).astype(jnp.bfloat16)
    keep_two = ((own_pos >= 2) & (prev_two == own_clip)).astype(jnp.bfloat16)
    start = jax.nn.silu(group_norm(latents.astype(jnp.float32), norm1_gain)).astype(jnp.bfloat16)
    hidden = causal_conv(start, conv1_weight, keep_one, keep_two).astype(jnp.bfloat16)
    middle = jax.nn.silu(group_norm(hidden.astype(jnp.float32), norm2_gain)).astype(jnp.bfloat16)
    update = causal_conv(middle, conv2_weight, keep_one, keep_two)
    resid = (latents.astype(jnp.float32) + update).astype(jnp.bfloat16)
    normed = group_norm(resid.astype(jnp.float32), norm3_gain).astype(jnp.bfloat16).reshape(-1, width)
    queries = jnp.dot(normed, query_weight, preferred_element_type=jnp.float32).astype(jnp.bfloat16)
    keys = jnp.dot(normed, key_weight, preferred_element_type=jnp.float32).astype(jnp.bfloat16)
    values = jnp.dot(normed, value_weight, preferred_element_type=jnp.float32).astype(jnp.bfloat16)
    slab = nframes // N_TM
    rows = slab * cells
    inner = queries.shape[1]
    padded_keys = jnp.concatenate([keys[keys.shape[0] - REACH * rows:], keys], axis=0)
    padded_values = jnp.concatenate([values[values.shape[0] - REACH * rows:], values], axis=0)
    scale = HEAD_DIM ** (-0.5)

    def one_block(index):
        query_block = lax.dynamic_slice_in_dim(queries, index * rows, rows, 0)
        key_block = lax.dynamic_slice_in_dim(padded_keys, index * rows, (REACH + 1) * rows, 0)
        value_block = lax.dynamic_slice_in_dim(padded_values, index * rows, (REACH + 1) * rows, 0)
        query_frames = index * slab + jnp.arange(slab, dtype=jnp.int32)
        key_frames = jnp.mod((index - REACH) * slab + jnp.arange((REACH + 1) * slab, dtype=jnp.int32), nframes).astype(jnp.int32)
        query_pos, query_clip = packed_place(query_frames, clip_lengths, nframes)
        key_pos, key_clip = packed_place(key_frames, clip_lengths, nframes)
        frame_mask = (key_clip[None, :] == query_clip[:, None]) & (key_pos[None, :] <= query_pos[:, None])
        allowed = jnp.broadcast_to(frame_mask[:, None, :, None], (slab, cells, (REACH + 1) * slab, cells)).reshape(rows, (REACH + 1) * rows)
        qh = query_block.reshape(rows, HEADS, HEAD_DIM).astype(jnp.float32)
        kh = key_block.reshape(-1, HEADS, HEAD_DIM).astype(jnp.float32)
        vh = value_block.reshape(-1, HEADS, HEAD_DIM).astype(jnp.float32)
        scores = jnp.einsum('qhd,khd->hqk', qh, kh, precision=lax.Precision.HIGHEST) * scale
        masked = jnp.where(allowed[None], scores, -1e+30)
        top = lax.optimization_barrier(jnp.max(masked, axis=-1, keepdims=True))
        weights = jnp.where(allowed[None], jnp.exp(scores - top), 0.0)
        rounded = weights.astype(jnp.bfloat16).astype(jnp.float32)
        numer = jnp.einsum('hqk,khd->hqd', rounded, vh, precision=lax.Precision.HIGHEST)
        result = numer / lax.optimization_barrier(jnp.sum(weights, axis=-1))[..., None]
        return jnp.transpose(result, (1, 0, 2)).reshape(rows, inner).astype(jnp.bfloat16)
    attended = lax.map(one_block, jnp.arange(N_TM, dtype=jnp.int32)).reshape(-1, inner)
    projected = jnp.dot(attended, out_weight, preferred_element_type=jnp.float32)
    encoded = resid.reshape(-1, width).astype(jnp.float32) + projected
    return encoded.astype(jnp.bfloat16).reshape(nframes, cells, width)
```

```python
import functools

import jax
import jax.numpy as jnp
from jax import lax
from jax.experimental import pallas as pl
from jax.experimental.pallas import tpu as pltpu
from jax.sharding import PartitionSpec as P

HEADS = 8
HEAD_DIM = 64
NORM_GROUPS = 32
HT = 8
WT = 16
CELLS = HT * WT
CLIP_MAX = 48
MASKED = -1e30
F32 = jnp.float32
BF16 = jnp.bfloat16
MESH = pl.DeviceIdType.MESH
VT_ROWS = HEAD_DIM + 16


def nt_dot(a, b):
    return lax.dot_general(a, b, (((1,), (1,)), ((), ())), preferred_element_type=F32)


def wrap(value, total):
    return jnp.where(value < 0, value + total, value)


def clip_table(clip_ref, total):
    ends = []
    run = jnp.int32(0)
    first = jnp.int32(0)
    found = jnp.int32(0)
    for k in range(clip_ref.shape[0]):
        length = clip_ref[k]
        hit = jnp.where(length == CLIP_MAX, 1, 0) * (1 - found)
        first = jnp.where(hit == 1, run, first)
        found = jnp.maximum(found, hit)
        run = run + length
        ends.append(run)
    shift = wrap(jnp.int32(total - CLIP_MAX // 2) - first, total)
    return ends, shift


def place(frame, ends, shift, total):
    pos = wrap(frame - shift, total)
    clip = jnp.zeros_like(pos)
    for end in ends:
        clip = clip + jnp.where(pos >= end, 1, 0)
    return pos, clip


def group_norm(frames_list, gain, same_group):
    width = frames_list[0].shape[1]
    count = CELLS * (width // NORM_GROUPS)
    pad = 8 - len(frames_list)

    def pooled(rows):
        stacked = jnp.concatenate(rows + [jnp.zeros((pad, width), F32)], axis=0)
        return jnp.dot(
            stacked, same_group, preferred_element_type=F32, precision=lax.Precision.HIGHEST
        ) * (1.0 / count)

    mean = pooled([jnp.sum(v, axis=0, keepdims=True) for v in frames_list])
    centred = [v - mean[i : i + 1] for i, v in enumerate(frames_list)]
    var = pooled([jnp.sum(v * v, axis=0, keepdims=True) for v in centred])
    inv = lax.rsqrt(var + 1e-6)
    return [v * inv[i : i + 1] * gain for i, v in enumerate(centred)]


def silu(v):
    return v / (1.0 + jnp.exp(-v))


def front_kernel(
    n,
    reach,
    lead,
    lat_ref,
    clip_ref,
    g1_ref,
    g2_ref,
    g3_ref,
    w1_hbm,
    w2_hbm,
    resid_ref,
    gath_ref,
    w1,
    w2,
    taps,
    halo1,
    halo2,
    edge1,
    edge2,
    acc,
    normed,
    w_sem,
    own_sem,
    hsend,
    hrecv,
    gsend,
    grecv,
):
    frames = lat_ref.shape[0]
    width = lat_ref.shape[2]
    total = frames * n
    me = lax.axis_index("tm")

    load1 = pltpu.make_async_copy(w1_hbm, w1, w_sem.at[0])
    load2 = pltpu.make_async_copy(w2_hbm, w2, w_sem.at[1])
    load1.start()
    load2.start()

    barrier = pltpu.get_barrier_semaphore()
    offsets = sorted({(s * d) % n for d in range(1, reach + 1) for s in (1, -1)} - {0})
    for off in offsets:
        pl.semaphore_signal(
            barrier, inc=1, device_id={"tm": lax.rem(me + off, n)}, device_id_type=MESH
        )

    def needs(target, d):
        rank = lax.rem(target + lead, n)
        return jnp.where(rank < reach, rank >= d, rank - reach >= d)

    ends, shift = clip_table(clip_ref, total)
    keep_one, keep_two = [], []
    for f in range(frames):
        g = me * frames + f
        pos, clip = place(g, ends, shift, total)
        clip1 = place(wrap(g - 1, total), ends, shift, total)[1]
        clip2 = place(wrap(g - 2, total), ends, shift, total)[1]
        keep_one.append(jnp.where((pos >= 1) & (clip1 == clip), 1.0, 0.0).astype(F32))
        keep_two.append(jnp.where((pos >= 2) & (clip2 == clip), 1.0, 0.0).astype(F32))

    li = lax.broadcasted_iota(jnp.int32, (width, width), 0) // (width // NORM_GROUPS)
    lj = lax.broadcasted_iota(jnp.int32, (width, width), 1) // (width // NORM_GROUPS)
    same_group = jnp.where(li == lj, 1.0, 0.0).astype(F32)
    col = lax.rem(lax.broadcasted_iota(jnp.int32, (CELLS, width), 0), WT)

    taps[:, :WT, :] = jnp.zeros((frames + 2, WT, 3 * width), BF16)
    taps[:, WT + CELLS :, :] = jnp.zeros((frames + 2, WT, 3 * width), BF16)

    def fill(f, v):
        left = jnp.where(col == 0, 0.0, pltpu.roll(v, 1, 0))
        right = jnp.where(col == WT - 1, 0.0, pltpu.roll(v, CELLS - 1, 0))
        rows = slice(WT, WT + CELLS)
        taps[f, rows, 0:width] = left.astype(BF16)
        taps[f, rows, width : 2 * width] = v.astype(BF16)
        taps[f, rows, 2 * width :] = right.astype(BF16)

    def product(w, dt):
        def step(dr, total_so_far):
            lhs = taps[dt : dt + frames, pl.ds(pl.multiple_of(dr * WT, WT), CELLS), :]
            lhs = lhs.reshape(frames * CELLS, 3 * width)
            rows = pl.multiple_of((dt * 3 + dr) * 3 * width, 3 * width)
            return total_so_far + jnp.dot(
                lhs, w[pl.ds(rows, 3 * width), :], preferred_element_type=F32
            )

        return lax.fori_loop(0, 3, step, jnp.zeros((frames * CELLS, width), F32))

    def conv(values, w, load, edge, halo, slot):
        for i in range(2):
            edge[i] = values[frames - 2 + i].astype(BF16)
        copy = pltpu.make_async_remote_copy(
            src_ref=edge,
            dst_ref=halo,
            send_sem=hsend.at[slot],
            recv_sem=hrecv.at[slot],
            device_id={"tm": lax.rem(me + 1, n)},
            device_id_type=MESH,
        )
        copy.start()
        for f in range(frames):
            fill(f + 2, values[f])
        load.wait()
        acc[...] = product(w, 2)
        copy.wait()
        for i in range(2):
            fill(i, halo[i].astype(F32))
        for dt, keep in ((1, keep_one), (0, keep_two)):
            part = product(w, dt)
            for f in range(frames):
                rows = slice(f * CELLS, (f + 1) * CELLS)
                acc[rows] += part[rows] * keep[f]
        return [acc[f * CELLS : (f + 1) * CELLS] for f in range(frames)]

    lat = [lat_ref[f].astype(F32) for f in range(frames)]
    start = [silu(v) for v in group_norm(lat, g1_ref[...], same_group)]
    pl.semaphore_wait(barrier, len(offsets))
    hidden = conv(start, w1, load1, edge1, halo1, 0)
    hidden = [v.astype(BF16).astype(F32) for v in hidden]
    middle = [silu(v) for v in group_norm(hidden, g2_ref[...], same_group)]
    update = conv(middle, w2, load2, edge2, halo2, 1)
    resid = [(lat_ref[f].astype(F32) + update[f]).astype(BF16) for f in range(frames)]
    for f in range(frames):
        resid_ref[f * CELLS : (f + 1) * CELLS] = resid[f]
    third = group_norm([v.astype(F32) for v in resid], g3_ref[...], same_group)
    for f in range(frames):
        normed[f * CELLS : (f + 1) * CELLS] = third[f].astype(BF16)

    own = pltpu.make_async_copy(normed, gath_ref.at[0], own_sem)
    own.start()

    def send(d):
        return pltpu.make_async_remote_copy(
            src_ref=normed,
            dst_ref=gath_ref.at[d],
            send_sem=gsend.at[d],
            recv_sem=grecv.at[d],
            device_id={"tm": lax.rem(me + d, n)},
            device_id_type=MESH,
        )

    for d in range(1, reach + 1):

        @pl.when(needs(lax.rem(me + d, n), d))
        def _(d=d):
            send(d).start()

    own.wait()
    for d in range(1, reach + 1):

        @pl.when(needs(lax.rem(me + d, n), d))
        def _(d=d):
            send(d).wait_send()

        @pl.when(needs(me, d))
        def _(d=d):
            send(d).wait_recv()


def attend_kernel(
    n,
    reach,
    lead,
    frames,
    gath_ref,
    resid_ref,
    clip_ref,
    wq_ref,
    wk_ref,
    wv_ref,
    wo_ref,
    out_ref,
    slab,
    qmat,
    kmat,
    vmat,
    wvt,
    top,
    acc,
    attended,
    sem,
):
    rows = frames * CELLS
    total = frames * n
    me = lax.axis_index("tm")
    pairs = HEADS // 2
    rank = lax.rem(me + lead, n)
    behind = jnp.minimum(jnp.where(rank < reach, rank, rank - reach), reach)

    def fetch(d, slot):
        return pltpu.make_async_copy(gath_ref.at[d], slab.at[slot], sem.at[slot])

    fetch(0, 0).start()
    ends, shift = clip_table(clip_ref, total)
    wvt[...] = wv_ref[...].astype(F32).T.astype(BF16)
    wqt = wq_ref[...].astype(F32).T.astype(BF16)
    top[...] = jnp.full(top.shape, MASKED, F32)
    acc[...] = jnp.zeros(acc.shape, F32)
    lane = lax.broadcasted_iota(jnp.int32, (16, 128), 1)
    q_pos, q_clip = place(me * frames + jnp.minimum(lane, frames - 1), ends, shift, total)
    fetch(0, 0).wait()

    qt = (nt_dot(wqt, slab[0]).astype(BF16).astype(F32) * HEAD_DIM ** (-0.5)).astype(BF16)
    row = lax.broadcasted_iota(jnp.int32, (128, 2 * rows), 0)
    colf = lax.rem(lax.broadcasted_iota(jnp.int32, (128, 2 * rows), 1), rows) // CELLS
    picks = jnp.where(row == colf, 1.0, 0.0).astype(BF16)
    blank = jnp.zeros((HEAD_DIM, rows), BF16)
    for p in range(pairs):
        base = 2 * p * HEAD_DIM
        qmat[p, 0:HEAD_DIM, 0:rows] = qt[base : base + HEAD_DIM]
        qmat[p, 0:HEAD_DIM, rows:] = blank
        qmat[p, HEAD_DIM:128, 0:rows] = blank
        qmat[p, HEAD_DIM:128, rows:] = qt[base + HEAD_DIM : base + 128]
        qmat[p, 128:256, :] = picks
    vmat[:, HEAD_DIM:, :] = jnp.ones((HEADS, VT_ROWS - HEAD_DIM, rows), BF16)

    @pl.loop(0, behind + 1)
    def _(d):
        slot = lax.rem(d, 2)

        @pl.when(d > 0)
        def _():
            fetch(d, slot).wait()

        @pl.when(d < behind)
        def _():
            fetch(d + 1, 1 - slot).start()

        block = slab[slot]
        keys = jnp.dot(block, wk_ref[...], preferred_element_type=F32).astype(BF16)
        for p in range(pairs):
            kmat[p, :, 0:128] = keys[:, p * 128 : (p + 1) * 128]
        source = wrap(me - d, n)
        for f in range(frames):
            k_pos, k_clip = place(source * frames + f, ends, shift, total)
            bias = jnp.where((q_clip == k_clip) & (q_pos >= k_pos), 0.0, MASKED).astype(BF16)
            for p in range(pairs):
                kmat[p, f * CELLS : (f + 1) * CELLS, 128:256] = jnp.broadcast_to(
                    bias[0:1], (CELLS, 128)
                )
        vt = nt_dot(wvt[...], block).astype(BF16)
        for h in range(HEADS):
            vmat[h, 0:HEAD_DIM, :] = vt[h * HEAD_DIM : (h + 1) * HEAD_DIM]

        @pl.loop(0, pairs)
        def _(p):
            for half in range(2):
                cols = slice(half * rows, (half + 1) * rows)
                scores = jnp.dot(kmat[p], qmat[p, :, cols], preferred_element_type=F32)
                old = top[p, :, cols]
                new = jnp.maximum(old, jnp.max(scores, axis=0, keepdims=True))
                weights = jnp.exp(scores - new[0:1]).astype(BF16)
                top[p, :, cols] = new
                acc[2 * p + half] = acc[2 * p + half] * jnp.exp(old - new)[0:1] + jnp.dot(
                    vmat[2 * p + half], weights, preferred_element_type=F32
                )

    for h in range(HEADS):
        part = acc[h, 0:HEAD_DIM] / acc[h, HEAD_DIM : HEAD_DIM + 1]
        attended[h * HEAD_DIM : (h + 1) * HEAD_DIM, :] = part
    att = attended[...].T.astype(BF16)
    projected = jnp.dot(att, wo_ref[...], preferred_element_type=F32)
    out_ref[...] = (resid_ref[...].astype(F32) + projected).astype(BF16)


def on_device(
    latents,
    clip_lengths,
    norm1_gain,
    conv1_weight,
    norm2_gain,
    conv2_weight,
    norm3_gain,
    query_weight,
    key_weight,
    value_weight,
    out_weight,
):
    frames, cells, width = latents.shape
    n = lax.axis_size("tm")
    reach = CLIP_MAX // frames
    lead = (CLIP_MAX // 2) // frames
    rows = frames * cells
    inner = HEADS * HEAD_DIM
    vmem = pl.BlockSpec(memory_space=pltpu.VMEM)
    smem = pl.BlockSpec(memory_space=pltpu.SMEM)
    hbm = pl.BlockSpec(memory_space=pl.ANY)

    resid, gathered = pl.pallas_call(
        functools.partial(front_kernel, n, reach, lead),
        out_shape=(
            jax.ShapeDtypeStruct((rows, width), BF16),
            jax.ShapeDtypeStruct((reach + 1, rows, width), BF16),
        ),
        in_specs=[vmem, smem, vmem, vmem, vmem, hbm, hbm],
        out_specs=(vmem, hbm),
        scratch_shapes=[
            pltpu.VMEM(conv1_weight.shape, BF16),
            pltpu.VMEM(conv2_weight.shape, BF16),
            pltpu.VMEM((frames + 2, cells + 2 * WT, 3 * width), BF16),
            pltpu.VMEM((2, cells, width), BF16),
            pltpu.VMEM((2, cells, width), BF16),
            pltpu.VMEM((2, cells, width), BF16),
            pltpu.VMEM((2, cells, width), BF16),
            pltpu.VMEM((rows, width), F32),
            pltpu.VMEM((rows, width), BF16),
            pltpu.SemaphoreType.DMA((2,)),
            pltpu.SemaphoreType.DMA,
            pltpu.SemaphoreType.DMA((2,)),
            pltpu.SemaphoreType.DMA((2,)),
            pltpu.SemaphoreType.DMA((reach + 1,)),
            pltpu.SemaphoreType.DMA((reach + 1,)),
        ],
        compiler_params=pltpu.CompilerParams(
            collective_id=0, has_side_effects=True, vmem_limit_bytes=48 << 20
        ),
    )(
        latents,
        clip_lengths,
        norm1_gain.reshape(1, width),
        norm2_gain.reshape(1, width),
        norm3_gain.reshape(1, width),
        conv1_weight,
        conv2_weight,
    )

    encoded = pl.pallas_call(
        functools.partial(attend_kernel, n, reach, lead, frames),
        out_shape=jax.ShapeDtypeStruct((rows, width), BF16),
        in_specs=[hbm, vmem, smem, vmem, vmem, vmem, vmem],
        out_specs=vmem,
        scratch_shapes=[
            pltpu.VMEM((2, rows, width), BF16),
            pltpu.VMEM((HEADS // 2, 256, 2 * rows), BF16),
            pltpu.VMEM((HEADS // 2, rows, 256), BF16),
            pltpu.VMEM((HEADS, VT_ROWS, rows), BF16),
            pltpu.VMEM((inner, width), BF16),
            pltpu.VMEM((HEADS // 2, 8, 2 * rows), F32),
            pltpu.VMEM((HEADS, VT_ROWS, rows), F32),
            pltpu.VMEM((inner, rows), F32),
            pltpu.SemaphoreType.DMA((2,)),
        ],
        compiler_params=pltpu.CompilerParams(vmem_limit_bytes=48 << 20),
    )(gathered, resid, clip_lengths, query_weight, key_weight, value_weight, out_weight)
    return encoded.reshape(frames, cells, width)


def solution(mesh):
    return jax.shard_map(
        on_device,
        mesh=mesh,
        in_specs=(P(("groups", "tm"), None, None), P("groups")) + (P(),) * 9,
        out_specs=P(("groups", "tm"), None, None),
        check_vma=False,
    )
```

```python
import functools

import jax
import jax.numpy as jnp
from jax import lax
from jax.experimental import pallas as pl
from jax.experimental.pallas import tpu as pltpu
from jax.sharding import PartitionSpec as P

HEADS = 8
HEAD_DIM = 64
NORM_GROUPS = 32
HT = 8
WT = 16
CELLS = HT * WT
CLIP_MAX = 48
MASKED = -1e30
F32 = jnp.float32
BF16 = jnp.bfloat16
MESH = pl.DeviceIdType.MESH
VT_ROWS = HEAD_DIM + 16


def nt_dot(a, b):
    return lax.dot_general(a, b, (((1,), (1,)), ((), ())), preferred_element_type=F32)


def wrap(value, total):
    return jnp.where(value < 0, value + total, value)


def clip_table(clip_ref, total):
    ends = []
    run = jnp.int32(0)
    first = jnp.int32(0)
    found = jnp.int32(0)
    for k in range(clip_ref.shape[0]):
        length = clip_ref[k]
        hit = jnp.where(length == CLIP_MAX, 1, 0) * (1 - found)
        first = jnp.where(hit == 1, run, first)
        found = jnp.maximum(found, hit)
        run = run + length
        ends.append(run)
    shift = wrap(jnp.int32(total - CLIP_MAX // 2) - first, total)
    return ends, shift


def place(frame, ends, shift, total):
    pos = wrap(frame - shift, total)
    clip = jnp.zeros_like(pos)
    for end in ends:
        clip = clip + jnp.where(pos >= end, 1, 0)
    return pos, clip


def group_norm(frames_list, gain, same_group):
    width = frames_list[0].shape[1]
    count = CELLS * (width // NORM_GROUPS)
    pad = 8 - len(frames_list)

    def pooled(rows):
        stacked = jnp.concatenate(rows + [jnp.zeros((pad, width), F32)], axis=0)
        return jnp.dot(
            stacked, same_group, preferred_element_type=F32, precision=lax.Precision.HIGHEST
        ) * (1.0 / count)

    mean = pooled([jnp.sum(v, axis=0, keepdims=True) for v in frames_list])
    centred = [v - mean[i : i + 1] for i, v in enumerate(frames_list)]
    var = pooled([jnp.sum(v * v, axis=0, keepdims=True) for v in centred])
    inv = lax.rsqrt(var + 1e-6)
    return [v * inv[i : i + 1] * gain for i, v in enumerate(centred)]


def silu(v):
    return v / (1.0 + jnp.exp(-v))


def block_kernel(
    n,
    reach,
    lead,
    lat_ref,
    clip_ref,
    g1_ref,
    g2_ref,
    g3_ref,
    w1_hbm,
    w2_hbm,
    wq_hbm,
    wk_hbm,
    wv_hbm,
    wo_hbm,
    out_ref,
    w1,
    w2,
    wq,
    wk,
    wv,
    wo,
    taps,
    halo1,
    halo2,
    edge1,
    edge2,
    conv_acc,
    resid_ref,
    slabs,
    qmat,
    kmat,
    vmat,
    wvt,
    wqt,
    top,
    acc,
    attended,
    back_o,
    back_s,
    home_o,
    home_s,
    w_sem,
    hsend,
    hrecv,
    rsend,
    rrecv,
    bsend,
    brecv,
    qsend,
    qrecv,
    osend,
    orecv,
):
    frames = lat_ref.shape[0]
    width = lat_ref.shape[2]
    rows = frames * CELLS
    total = frames * n
    pairs = HEADS // 2
    half = reach // 2
    back_base = reach + 1
    query_slot = back_base + half - 2
    me = lax.axis_index("tm")

    loads = []
    for i, (src, dst) in enumerate(
        ((w1_hbm, w1), (w2_hbm, w2), (wq_hbm, wq), (wk_hbm, wk), (wv_hbm, wv), (wo_hbm, wo))
    ):
        loads.append(pltpu.make_async_copy(src, dst, w_sem.at[i]))
        loads[i].start()

    barrier = pltpu.get_barrier_semaphore()
    offsets = sorted({(s * d) % n for d in range(1, reach + 1) for s in (1, -1)} - {0})
    for off in offsets:
        pl.semaphore_signal(
            barrier, inc=1, device_id={"tm": lax.rem(me + off, n)}, device_id_type=MESH
        )

    rank = lax.rem(me + lead, n)
    after = lax.rem(rank + 1, n)

    def depth(at):
        return jnp.where(
            at < reach, jnp.minimum(at, half), jnp.minimum(at - reach, reach)
        )

    behind = depth(rank)
    behind_next = depth(after)
    helps = rank < half - 1
    crossing = jnp.where(helps, half - 1 - rank, 0)
    before = jnp.maximum(1, 2 * rank - (half - 2))
    helped = (rank > half) & (rank < reach)
    mirror = lax.rem(me + reach - 1 - 2 * rank + 2 * n, n)

    ends, shift = clip_table(clip_ref, total)
    keep_one, keep_two = [], []
    for f in range(frames):
        g = me * frames + f
        pos, clip = place(g, ends, shift, total)
        clip1 = place(wrap(g - 1, total), ends, shift, total)[1]
        clip2 = place(wrap(g - 2, total), ends, shift, total)[1]
        keep_one.append(jnp.where((pos >= 1) & (clip1 == clip), 1.0, 0.0).astype(F32))
        keep_two.append(jnp.where((pos >= 2) & (clip2 == clip), 1.0, 0.0).astype(F32))

    li = lax.broadcasted_iota(jnp.int32, (width, width), 0) // (width // NORM_GROUPS)
    lj = lax.broadcasted_iota(jnp.int32, (width, width), 1) // (width // NORM_GROUPS)
    same_group = jnp.where(li == lj, 1.0, 0.0).astype(F32)
    col = lax.rem(lax.broadcasted_iota(jnp.int32, (CELLS, width), 0), WT)

    taps[:, :WT, :] = jnp.zeros((frames + 2, WT, 3 * width), BF16)
    taps[:, WT + CELLS :, :] = jnp.zeros((frames + 2, WT, 3 * width), BF16)

    def fill(f, v):
        left = jnp.where(col == 0, 0.0, pltpu.roll(v, 1, 0))
        right = jnp.where(col == WT - 1, 0.0, pltpu.roll(v, CELLS - 1, 0))
        rows = slice(WT, WT + CELLS)
        taps[f, rows, 0:width] = left.astype(BF16)
        taps[f, rows, width : 2 * width] = v.astype(BF16)
        taps[f, rows, 2 * width :] = right.astype(BF16)

    def product(w, dt):
        def step(dr, total_so_far):
            lhs = taps[dt : dt + frames, pl.ds(pl.multiple_of(dr * WT, WT), CELLS), :]
            lhs = lhs.reshape(frames * CELLS, 3 * width)
            rows = pl.multiple_of((dt * 3 + dr) * 3 * width, 3 * width)
            return total_so_far + jnp.dot(
                lhs, w[pl.ds(rows, 3 * width), :], preferred_element_type=F32
            )

        return lax.fori_loop(0, 3, step, jnp.zeros((frames * CELLS, width), F32))

    def conv(values, w, load, edge, halo, slot):
        for i in range(2):
            edge[i] = values[frames - 2 + i].astype(BF16)
        copy = pltpu.make_async_remote_copy(
            src_ref=edge,
            dst_ref=halo,
            send_sem=hsend.at[slot],
            recv_sem=hrecv.at[slot],
            device_id={"tm": lax.rem(me + 1, n)},
            device_id_type=MESH,
        )
        copy.start()
        for f in range(frames):
            fill(f + 2, values[f])
        load.wait()
        conv_acc[...] = product(w, 2)
        copy.wait()
        for i in range(2):
            fill(i, halo[i].astype(F32))
        for dt, keep in ((1, keep_one), (0, keep_two)):
            part = product(w, dt)
            for f in range(frames):
                rows = slice(f * CELLS, (f + 1) * CELLS)
                conv_acc[rows] += part[rows] * keep[f]
        return [conv_acc[f * CELLS : (f + 1) * CELLS] for f in range(frames)]

    lat = [lat_ref[f].astype(F32) for f in range(frames)]
    start = [silu(v) for v in group_norm(lat, g1_ref[...], same_group)]
    pl.semaphore_wait(barrier, len(offsets))
    hidden = conv(start, w1, loads[0], edge1, halo1, 0)
    hidden = [v.astype(BF16).astype(F32) for v in hidden]
    middle = [silu(v) for v in group_norm(hidden, g2_ref[...], same_group)]
    update = conv(middle, w2, loads[1], edge2, halo2, 1)
    resid = [(lat_ref[f].astype(F32) + update[f]).astype(BF16) for f in range(frames)]
    for f in range(frames):
        resid_ref[f * CELLS : (f + 1) * CELLS] = resid[f]
    third = group_norm([v.astype(F32) for v in resid], g3_ref[...], same_group)
    for f in range(frames):
        slabs[0, f * CELLS : (f + 1) * CELLS] = third[f].astype(BF16)

    def relay(d):
        return pltpu.make_async_remote_copy(
            src_ref=slabs.at[d],
            dst_ref=slabs.at[d + 1],
            send_sem=rsend.at[d],
            recv_sem=rrecv.at[d + 1],
            device_id={"tm": lax.rem(me + 1, n)},
            device_id_type=MESH,
        )

    def relay_in(d):
        return pltpu.make_async_remote_copy(
            src_ref=slabs.at[d],
            dst_ref=slabs.at[d],
            send_sem=rsend.at[d],
            recv_sem=rrecv.at[d],
            device_id={"tm": lax.rem(me + 1, n)},
            device_id_type=MESH,
        )

    def backward(d):
        return pltpu.make_async_remote_copy(
            src_ref=slabs.at[0],
            dst_ref=slabs.at[back_base + d - 1],
            send_sem=bsend.at[d],
            recv_sem=brecv.at[d],
            device_id={"tm": lax.rem(me - d + n, n)},
            device_id_type=MESH,
        )

    ask = pltpu.make_async_remote_copy(
        src_ref=slabs.at[0],
        dst_ref=slabs.at[query_slot],
        send_sem=qsend,
        recv_sem=qrecv,
        device_id={"tm": mirror},
        device_id_type=MESH,
    )

    def answers():
        return [
            pltpu.make_async_remote_copy(
                src_ref=src,
                dst_ref=dst,
                send_sem=osend.at[i],
                recv_sem=orecv.at[i],
                device_id={"tm": mirror},
                device_id_type=MESH,
            )
            for i, (src, dst) in enumerate(((back_o, home_o), (back_s, home_s)))
        ]

    @pl.when(behind_next >= 1)
    def _():
        relay(0).start()

    @pl.when(helped)
    def _():
        ask.start()

    def gives(d):
        return (rank >= d) & (2 * rank - d <= half - 2)

    def takes(d):
        return 2 * rank + d <= half - 2

    for d in range(1, half - 1):

        @pl.when(gives(d))
        def _(d=d):
            backward(d).start()

    for load in loads[2:]:
        load.wait()
    wvt[...] = wv[...].astype(F32).T.astype(BF16)
    wqt[...] = wq[...].astype(F32).T.astype(BF16)
    top[...] = jnp.full(top.shape, MASKED, F32)
    acc[...] = jnp.zeros(acc.shape, F32)
    vmat[:, HEAD_DIM:, :] = jnp.ones((HEADS, VT_ROWS - HEAD_DIM, rows), BF16)
    lane = jnp.minimum(lax.broadcasted_iota(jnp.int32, (16, 128), 1), frames - 1)
    row = lax.broadcasted_iota(jnp.int32, (128, 2 * rows), 0)
    colf = lax.rem(lax.broadcasted_iota(jnp.int32, (128, 2 * rows), 1), rows) // CELLS
    for which in range(2):
        for p in range(pairs):
            qmat[which, p, 128:256, :] = jnp.where(row == colf, 1.0, 0.0).astype(BF16)

    def set_queries(which, slot):
        qt = nt_dot(wqt[...], slabs[slot]).astype(BF16).astype(F32) * HEAD_DIM ** (-0.5)
        qt = qt.astype(BF16)
        blank = jnp.zeros((HEAD_DIM, rows), BF16)
        for p in range(pairs):
            base = 2 * p * HEAD_DIM
            qmat[which, p, 0:HEAD_DIM, 0:rows] = qt[base : base + HEAD_DIM]
            qmat[which, p, 0:HEAD_DIM, rows:] = blank
            qmat[which, p, HEAD_DIM:128, 0:rows] = blank
            qmat[which, p, HEAD_DIM:128, rows:] = qt[base + HEAD_DIM : base + 128]

    set_queries(0, 0)

    @pl.loop(0, behind + 1 + crossing)
    def _(t):
        @pl.when((t >= 1) & (t <= behind))
        def _():
            relay_in(t).wait_recv()

            @pl.when(t < behind_next)
            def _():
                relay(t).start()

        @pl.when((t == before) & helps)
        def _():
            ask.wait_recv()
            set_queries(1, query_slot)
            for d in range(1, half - 1):

                @pl.when(takes(d))
                def _(d=d):
                    backward(d).wait_recv()

        cross = (t >= before) & (t < before + crossing)
        which = jnp.where(cross, 1, 0)
        far = half - 2 - rank - (t - before)
        apart = jnp.where(cross, rank - far, jnp.where(t < before, t, t - crossing))
        slot = jnp.where(apart >= 0, apart, back_base - apart - 1)
        source = lax.rem(me - apart + n, n)
        asker = jnp.where(cross, mirror, me)
        q_pos, q_clip = place(asker * frames + lane, ends, shift, total)

        block = slabs[slot]
        keys = jnp.dot(block, wk[...], preferred_element_type=F32).astype(BF16)
        for p in range(pairs):
            kmat[p, :, 0:128] = keys[:, p * 128 : (p + 1) * 128]
        for f in range(frames):
            k_pos, k_clip = place(source * frames + f, ends, shift, total)
            bias = jnp.where((q_clip == k_clip) & (q_pos >= k_pos), 0.0, MASKED).astype(BF16)
            for p in range(pairs):
                kmat[p, f * CELLS : (f + 1) * CELLS, 128:256] = jnp.broadcast_to(
                    bias[0:1], (CELLS, 128)
                )
        vt = nt_dot(wvt[...], block).astype(BF16)
        for h in range(HEADS):
            vmat[h, 0:HEAD_DIM, :] = vt[h * HEAD_DIM : (h + 1) * HEAD_DIM]

        @pl.loop(0, pairs)
        def _(p):
            for side in range(2):
                cols = slice(side * rows, (side + 1) * rows)
                scores = jnp.dot(kmat[p], qmat[which, p, :, cols], preferred_element_type=F32)
                old = top[which, p, :, cols]
                new = jnp.maximum(old, jnp.max(scores, axis=0, keepdims=True))
                weights = jnp.exp(scores - new[0:1]).astype(BF16)
                top[which, p, :, cols] = new
                acc[which, 2 * p + side] = acc[which, 2 * p + side] * jnp.exp(old - new)[
                    0:1
                ] + jnp.dot(vmat[2 * p + side], weights, preferred_element_type=F32)

        @pl.when((t == before + crossing - 1) & helps)
        def _():
            for h in range(HEADS):
                cols = slice((h % 2) * rows, (h % 2 + 1) * rows)
                back_o[h] = acc[1, h, 0:HEAD_DIM].astype(BF16)
                back_s[0, h : h + 1] = top[1, h // 2, 0:1, cols]
                back_s[1, h : h + 1] = acc[1, h, HEAD_DIM : HEAD_DIM + 1]
            for copy in answers():
                copy.start()

    @pl.when(helped)
    def _():
        ask.wait_send()
        for copy in answers():
            copy.wait_recv()
        for h in range(HEADS):
            cols = slice((h % 2) * rows, (h % 2 + 1) * rows)
            mine = top[0, h // 2, 0:1, cols]
            theirs = home_s[0, h : h + 1]
            both = jnp.maximum(mine, theirs)
            scale_mine = jnp.exp(mine - both)
            scale_theirs = jnp.exp(theirs - both)
            acc[0, h, HEAD_DIM : HEAD_DIM + 1] = (
                acc[0, h, HEAD_DIM : HEAD_DIM + 1] * scale_mine
                + home_s[1, h : h + 1] * scale_theirs
            )
            acc[0, h, 0:HEAD_DIM] = (
                acc[0, h, 0:HEAD_DIM] * scale_mine + home_o[h].astype(F32) * scale_theirs
            )

    for h in range(HEADS):
        part = acc[0, h, 0:HEAD_DIM] / acc[0, h, HEAD_DIM : HEAD_DIM + 1]
        attended[h * HEAD_DIM : (h + 1) * HEAD_DIM, :] = part
    att = attended[...].T.astype(BF16)
    projected = jnp.dot(att, wo[...], preferred_element_type=F32)
    out_ref[...] = (resid_ref[...].astype(F32) + projected).astype(BF16)

    @pl.when(helps)
    def _():
        for copy in answers():
            copy.wait_send()

    for d in range(1, half - 1):

        @pl.when(gives(d))
        def _(d=d):
            backward(d).wait_send()

    @pl.loop(0, behind_next)
    def _(d):
        relay(d).wait_send()


def on_device(
    latents,
    clip_lengths,
    norm1_gain,
    conv1_weight,
    norm2_gain,
    conv2_weight,
    norm3_gain,
    query_weight,
    key_weight,
    value_weight,
    out_weight,
):
    frames, cells, width = latents.shape
    n = lax.axis_size("tm")
    reach = CLIP_MAX // frames
    lead = (CLIP_MAX // 2) // frames
    rows = frames * cells
    inner = HEADS * HEAD_DIM
    vmem = pl.BlockSpec(memory_space=pltpu.VMEM)
    smem = pl.BlockSpec(memory_space=pltpu.SMEM)
    hbm = pl.BlockSpec(memory_space=pl.ANY)
    dma = pltpu.SemaphoreType.DMA
    edge = pltpu.VMEM((2, cells, width), BF16)
    answer = pltpu.VMEM((HEADS, HEAD_DIM, rows), BF16)
    stats = pltpu.VMEM((2, HEADS, rows), F32)

    encoded = pl.pallas_call(
        functools.partial(block_kernel, n, reach, lead),
        out_shape=jax.ShapeDtypeStruct((rows, width), BF16),
        in_specs=[vmem, smem, vmem, vmem, vmem] + [hbm] * 6,
        out_specs=vmem,
        scratch_shapes=[
            pltpu.VMEM(conv1_weight.shape, BF16),
            pltpu.VMEM(conv2_weight.shape, BF16),
            pltpu.VMEM((width, inner), BF16),
            pltpu.VMEM((width, inner), BF16),
            pltpu.VMEM((width, inner), BF16),
            pltpu.VMEM((inner, width), BF16),
            pltpu.VMEM((frames + 2, cells + 2 * WT, 3 * width), BF16),
            edge,
            edge,
            edge,
            edge,
            pltpu.VMEM((rows, width), F32),
            pltpu.VMEM((rows, width), BF16),
            pltpu.VMEM((reach + reach // 2, rows, width), BF16),
            pltpu.VMEM((2, HEADS // 2, 256, 2 * rows), BF16),
            pltpu.VMEM((HEADS // 2, rows, 256), BF16),
            pltpu.VMEM((HEADS, VT_ROWS, rows), BF16),
            pltpu.VMEM((inner, width), BF16),
            pltpu.VMEM((inner, width), BF16),
            pltpu.VMEM((2, HEADS // 2, 8, 2 * rows), F32),
            pltpu.VMEM((2, HEADS, VT_ROWS, rows), F32),
            pltpu.VMEM((inner, rows), F32),
            answer,
            stats,
            answer,
            stats,
            dma((6,)),
            dma((2,)),
            dma((2,)),
            dma((reach + 1,)),
            dma((reach + 2,)),
            dma((reach // 2,)),
            dma((reach // 2,)),
            dma,
            dma,
            dma((2,)),
            dma((2,)),
        ],
        compiler_params=pltpu.CompilerParams(
            collective_id=0, has_side_effects=True, vmem_limit_bytes=56 << 20
        ),
    )(
        latents,
        clip_lengths,
        norm1_gain.reshape(1, width),
        norm2_gain.reshape(1, width),
        norm3_gain.reshape(1, width),
        conv1_weight,
        conv2_weight,
        query_weight,
        key_weight,
        value_weight,
        out_weight,
    )
    return encoded.reshape(frames, cells, width)


def solution(mesh):
    return jax.shard_map(
        on_device,
        mesh=mesh,
        in_specs=(P(("groups", "tm"), None, None), P("groups")) + (P(),) * 9,
        out_specs=P(("groups", "tm"), None, None),
        check_vma=False,
    )
```

```python
import functools

import jax
import jax.numpy as jnp
from jax import lax
from jax.experimental import pallas as pl
from jax.experimental.pallas import tpu as pltpu
from jax.sharding import PartitionSpec as P

HEADS = 8
HEAD_DIM = 64
NORM_GROUPS = 32
HT = 8
WT = 16
CELLS = HT * WT
CLIP_MAX = 48
MASKED = -1e30
F32 = jnp.float32
BF16 = jnp.bfloat16
MESH = pl.DeviceIdType.MESH
VT_ROWS = HEAD_DIM + 16


def nt_dot(a, b):
    return lax.dot_general(a, b, (((1,), (1,)), ((), ())), preferred_element_type=F32)


def wrap(value, total):
    return jnp.where(value < 0, value + total, value)


def clip_table(clip_ref, total):
    ends = []
    run = jnp.int32(0)
    first = jnp.int32(0)
    found = jnp.int32(0)
    for k in range(clip_ref.shape[0]):
        length = clip_ref[k]
        hit = jnp.where(length == CLIP_MAX, 1, 0) * (1 - found)
        first = jnp.where(hit == 1, run, first)
        found = jnp.maximum(found, hit)
        run = run + length
        ends.append(run)
    shift = wrap(jnp.int32(total - CLIP_MAX // 2) - first, total)
    return ends, shift


def place(frame, ends, shift, total):
    pos = wrap(frame - shift, total)
    clip = jnp.zeros_like(pos)
    for end in ends:
        clip = clip + jnp.where(pos >= end, 1, 0)
    return pos, clip


def group_norm(frames_list, gain, same_group):
    width = frames_list[0].shape[1]
    count = CELLS * (width // NORM_GROUPS)
    pad = 8 - len(frames_list)

    def pooled(rows):
        stacked = jnp.concatenate(rows + [jnp.zeros((pad, width), F32)], axis=0)
        return jnp.dot(
            stacked, same_group, preferred_element_type=F32, precision=lax.Precision.HIGHEST
        ) * (1.0 / count)

    mean = pooled([jnp.sum(v, axis=0, keepdims=True) for v in frames_list])
    centred = [v - mean[i : i + 1] for i, v in enumerate(frames_list)]
    var = pooled([jnp.sum(v * v, axis=0, keepdims=True) for v in centred])
    inv = lax.rsqrt(var + 1e-6)
    return [v * inv[i : i + 1] * gain for i, v in enumerate(centred)]


def silu(v):
    return v / (1.0 + jnp.exp(-v))


def block_kernel(
    n,
    reach,
    lead,
    lat_ref,
    clip_ref,
    g1_ref,
    g2_ref,
    g3_ref,
    w1_hbm,
    w2_hbm,
    wq_hbm,
    wk_hbm,
    wv_hbm,
    wo_hbm,
    out_ref,
    w1,
    w2,
    wq,
    wk,
    wv,
    wo,
    taps,
    halo1,
    halo2,
    edge1,
    edge2,
    conv_acc,
    resid_ref,
    slabs,
    qmat,
    kmat,
    vmat,
    wvt,
    wqt,
    top,
    acc,
    attended,
    back_o,
    back_s,
    home_o,
    home_s,
    w_sem,
    hsend,
    hrecv,
    rsend,
    rrecv,
    bsend,
    brecv,
    qsend,
    qrecv,
    osend,
    orecv,
):
    frames = lat_ref.shape[0]
    width = lat_ref.shape[2]
    rows = frames * CELLS
    total = frames * n
    pairs = HEADS // 2
    half = reach // 2
    back_base = reach + 1
    query_slot = back_base + half - 2
    me = lax.axis_index("tm")

    loads = []
    for i, (src, dst) in enumerate(
        ((w1_hbm, w1), (w2_hbm, w2), (wq_hbm, wq), (wk_hbm, wk), (wv_hbm, wv), (wo_hbm, wo))
    ):
        loads.append(pltpu.make_async_copy(src, dst, w_sem.at[i]))
        loads[i].start()

    barrier = pltpu.get_barrier_semaphore()
    offsets = sorted({(s * d) % n for d in range(1, reach + 1) for s in (1, -1)} - {0})
    for off in offsets:
        pl.semaphore_signal(
            barrier, inc=1, device_id={"tm": lax.rem(me + off, n)}, device_id_type=MESH
        )

    rank = lax.rem(me + lead, n)
    after = lax.rem(rank + 1, n)

    def depth(at):
        return jnp.where(
            at < reach, jnp.minimum(at, half), jnp.minimum(at - reach, reach)
        )

    behind = depth(rank)
    behind_next = depth(after)
    helps = rank < half - 1
    crossing = jnp.where(helps, half - 1 - rank, 0)
    before = jnp.maximum(1, 2 * rank - (half - 2))
    helped = (rank > half) & (rank < reach)
    ask_at = jnp.maximum(0, half + 3 - rank)
    mirror = lax.rem(me + reach - 1 - 2 * rank + 2 * n, n)

    ends, shift = clip_table(clip_ref, total)
    keep_one, keep_two = [], []
    for f in range(frames):
        g = me * frames + f
        pos, clip = place(g, ends, shift, total)
        clip1 = place(wrap(g - 1, total), ends, shift, total)[1]
        clip2 = place(wrap(g - 2, total), ends, shift, total)[1]
        keep_one.append(jnp.where((pos >= 1) & (clip1 == clip), 1.0, 0.0).astype(F32))
        keep_two.append(jnp.where((pos >= 2) & (clip2 == clip), 1.0, 0.0).astype(F32))

    li = lax.broadcasted_iota(jnp.int32, (width, width), 0) // (width // NORM_GROUPS)
    lj = lax.broadcasted_iota(jnp.int32, (width, width), 1) // (width // NORM_GROUPS)
    same_group = jnp.where(li == lj, 1.0, 0.0).astype(F32)
    col = lax.rem(lax.broadcasted_iota(jnp.int32, (CELLS, width), 0), WT)

    taps[:, :WT, :] = jnp.zeros((frames + 2, WT, 3 * width), BF16)
    taps[:, WT + CELLS :, :] = jnp.zeros((frames + 2, WT, 3 * width), BF16)

    def fill(f, v):
        left = jnp.where(col == 0, 0.0, pltpu.roll(v, 1, 0))
        right = jnp.where(col == WT - 1, 0.0, pltpu.roll(v, CELLS - 1, 0))
        rows = slice(WT, WT + CELLS)
        taps[f, rows, 0:width] = left.astype(BF16)
        taps[f, rows, width : 2 * width] = v.astype(BF16)
        taps[f, rows, 2 * width :] = right.astype(BF16)

    def product(w, dt):
        def step(dr, total_so_far):
            lhs = taps[dt : dt + frames, pl.ds(pl.multiple_of(dr * WT, WT), CELLS), :]
            lhs = lhs.reshape(frames * CELLS, 3 * width)
            rows = pl.multiple_of((dt * 3 + dr) * 3 * width, 3 * width)
            return total_so_far + jnp.dot(
                lhs, w[pl.ds(rows, 3 * width), :], preferred_element_type=F32
            )

        return lax.fori_loop(0, 3, step, jnp.zeros((frames * CELLS, width), F32))

    def conv(values, w, load, edge, halo, slot):
        for i in range(2):
            edge[i] = values[frames - 2 + i].astype(BF16)
        copy = pltpu.make_async_remote_copy(
            src_ref=edge,
            dst_ref=halo,
            send_sem=hsend.at[slot],
            recv_sem=hrecv.at[slot],
            device_id={"tm": lax.rem(me + 1, n)},
            device_id_type=MESH,
        )
        copy.start()
        for f in range(frames):
            fill(f + 2, values[f])
        load.wait()
        conv_acc[...] = product(w, 2)
        copy.wait()
        for i in range(2):
            fill(i, halo[i].astype(F32))
        for dt, keep in ((1, keep_one), (0, keep_two)):
            part = product(w, dt)
            for f in range(frames):
                rows = slice(f * CELLS, (f + 1) * CELLS)
                conv_acc[rows] += part[rows] * keep[f]
        return [conv_acc[f * CELLS : (f + 1) * CELLS] for f in range(frames)]

    lat = [lat_ref[f].astype(F32) for f in range(frames)]
    start = [silu(v) for v in group_norm(lat, g1_ref[...], same_group)]
    pl.semaphore_wait(barrier, len(offsets))
    hidden = conv(start, w1, loads[0], edge1, halo1, 0)
    hidden = [v.astype(BF16).astype(F32) for v in hidden]
    middle = [silu(v) for v in group_norm(hidden, g2_ref[...], same_group)]
    update = conv(middle, w2, loads[1], edge2, halo2, 1)
    resid = [(lat_ref[f].astype(F32) + update[f]).astype(BF16) for f in range(frames)]
    for f in range(frames):
        resid_ref[f * CELLS : (f + 1) * CELLS] = resid[f]
    third = group_norm([v.astype(F32) for v in resid], g3_ref[...], same_group)
    for f in range(frames):
        slabs[0, f * CELLS : (f + 1) * CELLS] = third[f].astype(BF16)

    def relay(d):
        return pltpu.make_async_remote_copy(
            src_ref=slabs.at[d],
            dst_ref=slabs.at[d + 1],
            send_sem=rsend.at[d],
            recv_sem=rrecv.at[d + 1],
            device_id={"tm": lax.rem(me + 1, n)},
            device_id_type=MESH,
        )

    def relay_in(d):
        return pltpu.make_async_remote_copy(
            src_ref=slabs.at[d],
            dst_ref=slabs.at[d],
            send_sem=rsend.at[d],
            recv_sem=rrecv.at[d],
            device_id={"tm": lax.rem(me + 1, n)},
            device_id_type=MESH,
        )

    def backward(d):
        return pltpu.make_async_remote_copy(
            src_ref=slabs.at[0],
            dst_ref=slabs.at[back_base + d - 1],
            send_sem=bsend.at[d],
            recv_sem=brecv.at[d],
            device_id={"tm": lax.rem(me - d + n, n)},
            device_id_type=MESH,
        )

    ask = pltpu.make_async_remote_copy(
        src_ref=slabs.at[0],
        dst_ref=slabs.at[query_slot],
        send_sem=qsend,
        recv_sem=qrecv,
        device_id={"tm": mirror},
        device_id_type=MESH,
    )

    def answers():
        return [
            pltpu.make_async_remote_copy(
                src_ref=src,
                dst_ref=dst,
                send_sem=osend.at[i],
                recv_sem=orecv.at[i],
                device_id={"tm": mirror},
                device_id_type=MESH,
            )
            for i, (src, dst) in enumerate(((back_o, home_o), (back_s, home_s)))
        ]

    @pl.when(behind_next >= 1)
    def _():
        relay(0).start()

    def gives(d):
        return (rank >= d) & (2 * rank - d <= half - 2)

    for d in range(1, half - 1):

        @pl.when(gives(d))
        def _(d=d):
            backward(d).start()

    for load in loads[2:]:
        load.wait()
    wvt[...] = wv[...].astype(F32).T.astype(BF16)
    wqt[...] = wq[...].astype(F32).T.astype(BF16)
    top[...] = jnp.full(top.shape, MASKED, F32)
    acc[...] = jnp.zeros(acc.shape, F32)
    vmat[:, HEAD_DIM:, :] = jnp.ones((HEADS, VT_ROWS - HEAD_DIM, rows), BF16)
    lane = jnp.minimum(lax.broadcasted_iota(jnp.int32, (16, 128), 1), frames - 1)
    row = lax.broadcasted_iota(jnp.int32, (128, 2 * rows), 0)
    colf = lax.rem(lax.broadcasted_iota(jnp.int32, (128, 2 * rows), 1), rows) // CELLS
    for which in range(2):
        for p in range(pairs):
            qmat[which, p, 128:256, :] = jnp.where(row == colf, 1.0, 0.0).astype(BF16)

    def set_queries(which, slot):
        qt = nt_dot(wqt[...], slabs[slot]).astype(BF16).astype(F32) * HEAD_DIM ** (-0.5)
        qt = qt.astype(BF16)
        blank = jnp.zeros((HEAD_DIM, rows), BF16)
        for p in range(pairs):
            base = 2 * p * HEAD_DIM
            qmat[which, p, 0:HEAD_DIM, 0:rows] = qt[base : base + HEAD_DIM]
            qmat[which, p, 0:HEAD_DIM, rows:] = blank
            qmat[which, p, HEAD_DIM:128, 0:rows] = blank
            qmat[which, p, HEAD_DIM:128, rows:] = qt[base + HEAD_DIM : base + 128]

    set_queries(0, 0)

    @pl.loop(0, behind + 1 + crossing)
    def _(t):
        @pl.when((t >= 1) & (t <= behind))
        def _():
            relay_in(t).wait_recv()

            @pl.when(t < behind_next)
            def _():
                relay(t).start()

        @pl.when(helped & (t == ask_at))
        def _():
            ask.start()

        @pl.when((t == before) & helps)
        def _():
            ask.wait_recv()
            set_queries(1, query_slot)

        cross = (t >= before) & (t < before + crossing)
        which = jnp.where(cross, 1, 0)
        nth = t - before
        nearest = jnp.minimum(rank, half - 2 - rank)
        far = jnp.where(nth <= nearest, nearest - nth, nth)
        apart = jnp.where(cross, rank - far, jnp.where(t < before, t, t - crossing))
        slot = jnp.where(apart >= 0, apart, back_base - apart - 1)
        source = lax.rem(me - apart + n, n)
        asker = jnp.where(cross, mirror, me)
        q_pos, q_clip = place(asker * frames + lane, ends, shift, total)

        @pl.when(cross & (apart < 0))
        def _():
            backward(-apart).wait_recv()

        block = slabs[slot]
        keys = jnp.dot(block, wk[...], preferred_element_type=F32).astype(BF16)
        for p in range(pairs):
            kmat[p, :, 0:128] = keys[:, p * 128 : (p + 1) * 128]
        for f in range(frames):
            k_pos, k_clip = place(source * frames + f, ends, shift, total)
            bias = jnp.where((q_clip == k_clip) & (q_pos >= k_pos), 0.0, MASKED).astype(BF16)
            for p in range(pairs):
                kmat[p, f * CELLS : (f + 1) * CELLS, 128:256] = jnp.broadcast_to(
                    bias[0:1], (CELLS, 128)
                )
        vt = nt_dot(wvt[...], block).astype(BF16)
        for h in range(HEADS):
            vmat[h, 0:HEAD_DIM, :] = vt[h * HEAD_DIM : (h + 1) * HEAD_DIM]

        def score(h):
            cols = slice((h % 2) * rows, (h % 2 + 1) * rows)
            return jnp.dot(
                kmat[h // 2], qmat[which, h // 2, :, cols], preferred_element_type=F32
            )

        coming = score(0)
        for h in range(HEADS):
            scores = coming
            if h + 1 < HEADS:
                coming = score(h + 1)
            cols = slice((h % 2) * rows, (h % 2 + 1) * rows)
            old = top[which, h // 2, :, cols]
            new = jnp.maximum(old, jnp.max(scores, axis=0, keepdims=True))
            weights = jnp.exp(scores - new[0:1]).astype(BF16)
            top[which, h // 2, :, cols] = new
            acc[which, h] = acc[which, h] * jnp.exp(old - new)[0:1] + jnp.dot(
                vmat[h], weights, preferred_element_type=F32
            )

        @pl.when((t == before + crossing - 1) & helps)
        def _():
            for h in range(HEADS):
                cols = slice((h % 2) * rows, (h % 2 + 1) * rows)
                back_o[h] = acc[1, h, 0:HEAD_DIM].astype(BF16)
                back_s[0, h : h + 1] = top[1, h // 2, 0:1, cols]
                back_s[1, h : h + 1] = acc[1, h, HEAD_DIM : HEAD_DIM + 1]
            for copy in answers():
                copy.start()

    @pl.when(helped)
    def _():
        ask.wait_send()
        for copy in answers():
            copy.wait_recv()
        for h in range(HEADS):
            cols = slice((h % 2) * rows, (h % 2 + 1) * rows)
            mine = top[0, h // 2, 0:1, cols]
            theirs = home_s[0, h : h + 1]
            both = jnp.maximum(mine, theirs)
            scale_mine = jnp.exp(mine - both)
            scale_theirs = jnp.exp(theirs - both)
            acc[0, h, HEAD_DIM : HEAD_DIM + 1] = (
                acc[0, h, HEAD_DIM : HEAD_DIM + 1] * scale_mine
                + home_s[1, h : h + 1] * scale_theirs
            )
            acc[0, h, 0:HEAD_DIM] = (
                acc[0, h, 0:HEAD_DIM] * scale_mine + home_o[h].astype(F32) * scale_theirs
            )

    for h in range(HEADS):
        part = acc[0, h, 0:HEAD_DIM] / acc[0, h, HEAD_DIM : HEAD_DIM + 1]
        attended[h * HEAD_DIM : (h + 1) * HEAD_DIM, :] = part
    att = attended[...].T.astype(BF16)
    projected = jnp.dot(att, wo[...], preferred_element_type=F32)
    out_ref[...] = (resid_ref[...].astype(F32) + projected).astype(BF16)

    @pl.when(helps)
    def _():
        for copy in answers():
            copy.wait_send()

    for d in range(1, half - 1):

        @pl.when(gives(d))
        def _(d=d):
            backward(d).wait_send()

    @pl.loop(0, behind_next)
    def _(d):
        relay(d).wait_send()


def on_device(
    latents,
    clip_lengths,
    norm1_gain,
    conv1_weight,
    norm2_gain,
    conv2_weight,
    norm3_gain,
    query_weight,
    key_weight,
    value_weight,
    out_weight,
):
    frames, cells, width = latents.shape
    n = lax.axis_size("tm")
    reach = CLIP_MAX // frames
    lead = (CLIP_MAX // 2) // frames
    rows = frames * cells
    inner = HEADS * HEAD_DIM
    vmem = pl.BlockSpec(memory_space=pltpu.VMEM)
    smem = pl.BlockSpec(memory_space=pltpu.SMEM)
    hbm = pl.BlockSpec(memory_space=pl.ANY)
    dma = pltpu.SemaphoreType.DMA
    edge = pltpu.VMEM((2, cells, width), BF16)
    answer = pltpu.VMEM((HEADS, HEAD_DIM, rows), BF16)
    stats = pltpu.VMEM((2, HEADS, rows), F32)

    encoded = pl.pallas_call(
        functools.partial(block_kernel, n, reach, lead),
        out_shape=jax.ShapeDtypeStruct((rows, width), BF16),
        in_specs=[vmem, smem, vmem, vmem, vmem] + [hbm] * 6,
        out_specs=vmem,
        scratch_shapes=[
            pltpu.VMEM(conv1_weight.shape, BF16),
            pltpu.VMEM(conv2_weight.shape, BF16),
            pltpu.VMEM((width, inner), BF16),
            pltpu.VMEM((width, inner), BF16),
            pltpu.VMEM((width, inner), BF16),
            pltpu.VMEM((inner, width), BF16),
            pltpu.VMEM((frames + 2, cells + 2 * WT, 3 * width), BF16),
            edge,
            edge,
            edge,
            edge,
            pltpu.VMEM((rows, width), F32),
            pltpu.VMEM((rows, width), BF16),
            pltpu.VMEM((reach + reach // 2, rows, width), BF16),
            pltpu.VMEM((2, HEADS // 2, 256, 2 * rows), BF16),
            pltpu.VMEM((HEADS // 2, rows, 256), BF16),
            pltpu.VMEM((HEADS, VT_ROWS, rows), BF16),
            pltpu.VMEM((inner, width), BF16),
            pltpu.VMEM((inner, width), BF16),
            pltpu.VMEM((2, HEADS // 2, 8, 2 * rows), F32),
            pltpu.VMEM((2, HEADS, VT_ROWS, rows), F32),
            pltpu.VMEM((inner, rows), F32),
            answer,
            stats,
            answer,
            stats,
            dma((6,)),
            dma((2,)),
            dma((2,)),
            dma((reach + 1,)),
            dma((reach + 2,)),
            dma((reach // 2,)),
            dma((reach // 2,)),
            dma,
            dma,
            dma((2,)),
            dma((2,)),
        ],
        compiler_params=pltpu.CompilerParams(
            collective_id=0, has_side_effects=True, vmem_limit_bytes=56 << 20
        ),
    )(
        latents,
        clip_lengths,
        norm1_gain.reshape(1, width),
        norm2_gain.reshape(1, width),
        norm3_gain.reshape(1, width),
        conv1_weight,
        conv2_weight,
        query_weight,
        key_weight,
        value_weight,
        out_weight,
    )
    return encoded.reshape(frames, cells, width)


def solution(mesh):
    return jax.shard_map(
        on_device,
        mesh=mesh,
        in_specs=(P(("groups", "tm"), None, None), P("groups")) + (P(),) * 9,
        out_specs=P(("groups", "tm"), None, None),
        check_vma=False,
    )
```

```python
import functools

import jax
import jax.numpy as jnp
from jax import lax
from jax.experimental import pallas as pl
from jax.experimental.pallas import tpu as pltpu
from jax.sharding import PartitionSpec as P

HEADS = 8
HEAD_DIM = 64
NORM_GROUPS = 32
HT = 8
WT = 16
CELLS = HT * WT
CLIP_MAX = 48
MASKED = -1e30
F32 = jnp.float32
BF16 = jnp.bfloat16
MESH = pl.DeviceIdType.MESH
VT_ROWS = HEAD_DIM + 16


def nt_dot(a, b):
    return lax.dot_general(a, b, (((1,), (1,)), ((), ())), preferred_element_type=F32)


def wrap(value, total):
    return jnp.where(value < 0, value + total, value)


def clip_table(clip_ref, total):
    ends = []
    run = jnp.int32(0)
    first = jnp.int32(0)
    found = jnp.int32(0)
    for k in range(clip_ref.shape[0]):
        length = clip_ref[k]
        hit = jnp.where(length == CLIP_MAX, 1, 0) * (1 - found)
        first = jnp.where(hit == 1, run, first)
        found = jnp.maximum(found, hit)
        run = run + length
        ends.append(run)
    shift = wrap(jnp.int32(total - CLIP_MAX // 2) - first, total)
    return ends, shift


def place(frame, ends, shift, total):
    pos = wrap(frame - shift, total)
    clip = jnp.zeros_like(pos)
    for end in ends:
        clip = clip + jnp.where(pos >= end, 1, 0)
    return pos, clip


def group_norm(frames_list, gain, same_group):
    width = frames_list[0].shape[1]
    count = CELLS * (width // NORM_GROUPS)
    pad = 8 - len(frames_list)

    def pooled(rows):
        stacked = jnp.concatenate(rows + [jnp.zeros((pad, width), F32)], axis=0)
        return jnp.dot(
            stacked, same_group, preferred_element_type=F32, precision=lax.Precision.HIGHEST
        ) * (1.0 / count)

    mean = pooled([jnp.sum(v, axis=0, keepdims=True) for v in frames_list])
    centred = [v - mean[i : i + 1] for i, v in enumerate(frames_list)]
    var = pooled([jnp.sum(v * v, axis=0, keepdims=True) for v in centred])
    inv = lax.rsqrt(var + 1e-6)
    return [v * inv[i : i + 1] * gain for i, v in enumerate(centred)]


def silu(v):
    return v / (1.0 + jnp.exp(-v))


def block_kernel(
    n,
    reach,
    lead,
    lat_ref,
    clip_ref,
    g1_ref,
    g2_ref,
    g3_ref,
    w1_hbm,
    w2_hbm,
    wq_hbm,
    wk_hbm,
    wv_hbm,
    wo_hbm,
    out_ref,
    w1,
    w2,
    wq,
    wk,
    wv,
    wo,
    taps,
    halo1,
    halo2,
    edge1,
    edge2,
    conv_acc,
    resid_ref,
    slabs,
    qmat,
    kmat,
    vmat,
    wvt,
    wqt,
    top,
    acc,
    attended,
    back_o,
    back_s,
    home_o,
    home_s,
    w_sem,
    hsend,
    hrecv,
    rsend,
    rrecv,
    bsend,
    brecv,
    tsend,
    qsend,
    qrecv,
    osend,
    orecv,
):
    frames = lat_ref.shape[0]
    width = lat_ref.shape[2]
    rows = frames * CELLS
    total = frames * n
    pairs = HEADS // 2
    half = reach // 2
    back_base = reach + 1
    query_slot = back_base + half - 2
    me = lax.axis_index("tm")

    loads = []
    for i, (src, dst) in enumerate(
        ((w1_hbm, w1), (w2_hbm, w2), (wq_hbm, wq), (wk_hbm, wk), (wv_hbm, wv), (wo_hbm, wo))
    ):
        loads.append(pltpu.make_async_copy(src, dst, w_sem.at[i]))
        loads[i].start()

    barrier = pltpu.get_barrier_semaphore()
    offsets = sorted({(s * d) % n for d in range(1, reach + 1) for s in (1, -1)} - {0})
    for off in offsets:
        pl.semaphore_signal(
            barrier, inc=1, device_id={"tm": lax.rem(me + off, n)}, device_id_type=MESH
        )

    rank = lax.rem(me + lead, n)
    after = lax.rem(rank + 1, n)

    def depth(at):
        return jnp.where(
            at < reach, jnp.minimum(at, half), jnp.minimum(at - reach, reach)
        )

    behind = depth(rank)
    behind_next = depth(after)
    helps = rank < half - 1
    crossing = jnp.where(helps, half - 1 - rank, 0)
    later = jnp.maximum(half - 2 - 2 * rank, 0)
    before = jnp.maximum(1, 2 * rank - (half - 2))
    helped = (rank > half) & (rank < reach)
    ask_at = jnp.maximum(0, half + 3 - rank)
    mirror = lax.rem(me + reach - 1 - 2 * rank + 2 * n, n)

    ends, shift = clip_table(clip_ref, total)
    keep_one, keep_two = [], []
    for f in range(frames):
        g = me * frames + f
        pos, clip = place(g, ends, shift, total)
        clip1 = place(wrap(g - 1, total), ends, shift, total)[1]
        clip2 = place(wrap(g - 2, total), ends, shift, total)[1]
        keep_one.append(jnp.where((pos >= 1) & (clip1 == clip), 1.0, 0.0).astype(F32))
        keep_two.append(jnp.where((pos >= 2) & (clip2 == clip), 1.0, 0.0).astype(F32))

    li = lax.broadcasted_iota(jnp.int32, (width, width), 0) // (width // NORM_GROUPS)
    lj = lax.broadcasted_iota(jnp.int32, (width, width), 1) // (width // NORM_GROUPS)
    same_group = jnp.where(li == lj, 1.0, 0.0).astype(F32)
    col = lax.rem(lax.broadcasted_iota(jnp.int32, (CELLS, width), 0), WT)

    taps[:, :WT, :] = jnp.zeros((frames + 2, WT, 3 * width), BF16)
    taps[:, WT + CELLS :, :] = jnp.zeros((frames + 2, WT, 3 * width), BF16)

    def fill(f, v):
        left = jnp.where(col == 0, 0.0, pltpu.roll(v, 1, 0))
        right = jnp.where(col == WT - 1, 0.0, pltpu.roll(v, CELLS - 1, 0))
        rows = slice(WT, WT + CELLS)
        taps[f, rows, 0:width] = left.astype(BF16)
        taps[f, rows, width : 2 * width] = v.astype(BF16)
        taps[f, rows, 2 * width :] = right.astype(BF16)

    def product(w, dt):
        def step(dr, total_so_far):
            lhs = taps[dt : dt + frames, pl.ds(pl.multiple_of(dr * WT, WT), CELLS), :]
            lhs = lhs.reshape(frames * CELLS, 3 * width)
            rows = pl.multiple_of((dt * 3 + dr) * 3 * width, 3 * width)
            return total_so_far + jnp.dot(
                lhs, w[pl.ds(rows, 3 * width), :], preferred_element_type=F32
            )

        return lax.fori_loop(0, 3, step, jnp.zeros((frames * CELLS, width), F32))

    def conv(values, w, load, edge, halo, slot):
        for i in range(2):
            edge[i] = values[frames - 2 + i].astype(BF16)
        copy = pltpu.make_async_remote_copy(
            src_ref=edge,
            dst_ref=halo,
            send_sem=hsend.at[slot],
            recv_sem=hrecv.at[slot],
            device_id={"tm": lax.rem(me + 1, n)},
            device_id_type=MESH,
        )
        copy.start()
        for f in range(frames):
            fill(f + 2, values[f])
        load.wait()
        conv_acc[...] = product(w, 2)
        copy.wait()
        for i in range(2):
            fill(i, halo[i].astype(F32))
        for dt, keep in ((1, keep_one), (0, keep_two)):
            part = product(w, dt)
            for f in range(frames):
                rows = slice(f * CELLS, (f + 1) * CELLS)
                conv_acc[rows] += part[rows] * keep[f]
        return [conv_acc[f * CELLS : (f + 1) * CELLS] for f in range(frames)]

    lat = [lat_ref[f].astype(F32) for f in range(frames)]
    start = [silu(v) for v in group_norm(lat, g1_ref[...], same_group)]
    pl.semaphore_wait(barrier, len(offsets))
    hidden = conv(start, w1, loads[0], edge1, halo1, 0)
    hidden = [v.astype(BF16).astype(F32) for v in hidden]
    middle = [silu(v) for v in group_norm(hidden, g2_ref[...], same_group)]
    update = conv(middle, w2, loads[1], edge2, halo2, 1)
    resid = [(lat_ref[f].astype(F32) + update[f]).astype(BF16) for f in range(frames)]
    for f in range(frames):
        resid_ref[f * CELLS : (f + 1) * CELLS] = resid[f]
    third = group_norm([v.astype(F32) for v in resid], g3_ref[...], same_group)
    for f in range(frames):
        slabs[0, f * CELLS : (f + 1) * CELLS] = third[f].astype(BF16)

    def relay(d):
        return pltpu.make_async_remote_copy(
            src_ref=slabs.at[d],
            dst_ref=slabs.at[d + 1],
            send_sem=rsend.at[d],
            recv_sem=rrecv.at[d + 1],
            device_id={"tm": lax.rem(me + 1, n)},
            device_id_type=MESH,
        )

    def relay_in(d):
        return pltpu.make_async_remote_copy(
            src_ref=slabs.at[d],
            dst_ref=slabs.at[d],
            send_sem=rsend.at[d],
            recv_sem=rrecv.at[d],
            device_id={"tm": lax.rem(me + 1, n)},
            device_id_type=MESH,
        )

    def backward(d):
        return pltpu.make_async_remote_copy(
            src_ref=slabs.at[0],
            dst_ref=slabs.at[back_base + d - 1],
            send_sem=bsend.at[d],
            recv_sem=brecv.at[d],
            device_id={"tm": lax.rem(me - d + n, n)},
            device_id_type=MESH,
        )

    ask = pltpu.make_async_remote_copy(
        src_ref=slabs.at[0],
        dst_ref=slabs.at[query_slot],
        send_sem=qsend,
        recv_sem=qrecv,
        device_id={"tm": mirror},
        device_id_type=MESH,
    )

    def answer(i):
        first, second = slice(0, HEADS // 2), slice(HEADS // 2, HEADS)
        src, dst = (
            (back_o.at[first], home_o.at[first]),
            (back_o.at[second], home_o.at[second]),
            (back_s, home_s),
        )[i]
        return pltpu.make_async_remote_copy(
            src_ref=src,
            dst_ref=dst,
            send_sem=osend.at[i],
            recv_sem=orecv.at[i],
            device_id={"tm": mirror},
            device_id_type=MESH,
        )

    @pl.when(behind_next >= 1)
    def _():
        relay(0).start()

    def gives(d):
        to = rank - d
        passed = (lax.rem(to, 2) == 0) & (to + 1 < rank) & (rank + to + 1 <= half - 2)
        return (to >= 0) & (rank + to <= half - 2) & jnp.logical_not(passed)

    hands_on = helps & (lax.rem(rank, 2) == 1)

    def hand_on(d):
        return pltpu.make_async_remote_copy(
            src_ref=slabs.at[back_base + d - 1],
            dst_ref=slabs.at[back_base + d],
            send_sem=tsend.at[d],
            recv_sem=brecv.at[d + 1],
            device_id={"tm": lax.rem(me - 1 + n, n)},
            device_id_type=MESH,
        )

    for d in range(1, half - 1):

        @pl.when(gives(d))
        def _(d=d):
            backward(d).start()

    for load in loads[2:]:
        load.wait()
    wvt[...] = wv[...].astype(F32).T.astype(BF16)
    wqt[...] = wq[...].astype(F32).T.astype(BF16)
    top[...] = jnp.full(top.shape, MASKED, F32)
    acc[...] = jnp.zeros(acc.shape, F32)
    vmat[:, HEAD_DIM:, :] = jnp.ones((HEADS, VT_ROWS - HEAD_DIM, rows), BF16)
    lane = jnp.minimum(lax.broadcasted_iota(jnp.int32, (16, 128), 1), frames - 1)
    row = lax.broadcasted_iota(jnp.int32, (128, 2 * rows), 0)
    colf = lax.rem(lax.broadcasted_iota(jnp.int32, (128, 2 * rows), 1), rows) // CELLS
    for which in range(2):
        for p in range(pairs):
            qmat[which, p, 128:256, :] = jnp.where(row == colf, 1.0, 0.0).astype(BF16)

    def set_queries(which, slot):
        qt = nt_dot(wqt[...], slabs[slot]).astype(BF16).astype(F32) * HEAD_DIM ** (-0.5)
        qt = qt.astype(BF16)
        blank = jnp.zeros((HEAD_DIM, rows), BF16)
        for p in range(pairs):
            base = 2 * p * HEAD_DIM
            qmat[which, p, 0:HEAD_DIM, 0:rows] = qt[base : base + HEAD_DIM]
            qmat[which, p, 0:HEAD_DIM, rows:] = blank
            qmat[which, p, HEAD_DIM:128, 0:rows] = blank
            qmat[which, p, HEAD_DIM:128, rows:] = qt[base + HEAD_DIM : base + 128]

    set_queries(0, 0)

    def answer_part(heads, copies, ready):
        @pl.when(ready)
        def _():
            for h in heads:
                cols = slice((h % 2) * rows, (h % 2 + 1) * rows)
                back_o[h] = acc[1, h, 0:HEAD_DIM].astype(BF16)
                back_s[0, h : h + 1] = top[1, h // 2, 0:1, cols]
                back_s[1, h : h + 1] = acc[1, h, HEAD_DIM : HEAD_DIM + 1]
            for i in copies:
                answer(i).start()

    @pl.loop(0, behind + 1 + crossing)
    def _(t):
        @pl.when((t >= 1) & (t <= behind))
        def _():
            relay_in(t).wait_recv()

            @pl.when(t < behind_next)
            def _():
                relay(t).start()

        @pl.when(helped & (t == ask_at))
        def _():
            ask.start()

        @pl.when((t == before) & helps)
        def _():
            ask.wait_recv()
            set_queries(1, query_slot)

        cross = (t >= before) & (t < before + crossing)
        which = jnp.where(cross, 1, 0)
        nth = t - before
        nearest = jnp.minimum(rank, half - 2 - rank)
        far = jnp.where(nth <= later, nearest + nth, nearest - (nth - later))
        apart = jnp.where(cross, rank - far, jnp.where(t < before, t, t - crossing))
        slot = jnp.where(apart >= 0, apart, back_base - apart - 1)
        source = lax.rem(me - apart + n, n)
        asker = jnp.where(cross, mirror, me)
        q_pos, q_clip = place(asker * frames + lane, ends, shift, total)

        @pl.when(cross & (apart < 0))
        def _():
            backward(-apart).wait_recv()

            @pl.when(hands_on)
            def _():
                hand_on(-apart).start()

        block = slabs[slot]
        keys = jnp.dot(block, wk[...], preferred_element_type=F32).astype(BF16)
        for p in range(pairs):
            kmat[p, :, 0:128] = keys[:, p * 128 : (p + 1) * 128]
        for f in range(frames):
            k_pos, k_clip = place(source * frames + f, ends, shift, total)
            bias = jnp.where((q_clip == k_clip) & (q_pos >= k_pos), 0.0, MASKED).astype(BF16)
            for p in range(pairs):
                kmat[p, f * CELLS : (f + 1) * CELLS, 128:256] = jnp.broadcast_to(
                    bias[0:1], (CELLS, 128)
                )
        vt = nt_dot(wvt[...], block).astype(BF16)
        for h in range(HEADS):
            vmat[h, 0:HEAD_DIM, :] = vt[h * HEAD_DIM : (h + 1) * HEAD_DIM]

        def score(h):
            cols = slice((h % 2) * rows, (h % 2 + 1) * rows)
            return jnp.dot(
                kmat[h // 2], qmat[which, h // 2, :, cols], preferred_element_type=F32
            )

        last = (t == before + crossing - 1) & helps

        coming = score(0)
        for h in range(HEADS):
            scores = coming
            if h + 1 < HEADS:
                coming = score(h + 1)
            cols = slice((h % 2) * rows, (h % 2 + 1) * rows)
            old = top[which, h // 2, :, cols]
            new = jnp.maximum(old, jnp.max(scores, axis=0, keepdims=True))
            weights = jnp.exp(scores - new[0:1]).astype(BF16)
            top[which, h // 2, :, cols] = new
            acc[which, h] = acc[which, h] * jnp.exp(old - new)[0:1] + jnp.dot(
                vmat[h], weights, preferred_element_type=F32
            )
            if h == HEADS // 2 - 1:
                answer_part(range(HEADS // 2), (0,), last)
            if h == HEADS - 1:
                answer_part(range(HEADS // 2, HEADS), (1, 2), last)

    @pl.when(helped)
    def _():
        ask.wait_send()
        for i in range(3):
            answer(i).wait_recv()
        for h in range(HEADS):
            cols = slice((h % 2) * rows, (h % 2 + 1) * rows)
            mine = top[0, h // 2, 0:1, cols]
            theirs = home_s[0, h : h + 1]
            both = jnp.maximum(mine, theirs)
            scale_mine = jnp.exp(mine - both)
            scale_theirs = jnp.exp(theirs - both)
            acc[0, h, HEAD_DIM : HEAD_DIM + 1] = (
                acc[0, h, HEAD_DIM : HEAD_DIM + 1] * scale_mine
                + home_s[1, h : h + 1] * scale_theirs
            )
            acc[0, h, 0:HEAD_DIM] = (
                acc[0, h, 0:HEAD_DIM] * scale_mine + home_o[h].astype(F32) * scale_theirs
            )

    for h in range(HEADS):
        part = acc[0, h, 0:HEAD_DIM] / acc[0, h, HEAD_DIM : HEAD_DIM + 1]
        attended[h * HEAD_DIM : (h + 1) * HEAD_DIM, :] = part
    att = attended[...].T.astype(BF16)
    projected = jnp.dot(att, wo[...], preferred_element_type=F32)
    out_ref[...] = (resid_ref[...].astype(F32) + projected).astype(BF16)

    @pl.when(helps)
    def _():
        for i in range(3):
            answer(i).wait_send()

    for d in range(1, half - 1):

        @pl.when(gives(d))
        def _(d=d):
            backward(d).wait_send()

    @pl.when(hands_on)
    def _():
        @pl.loop(1, later + 1)
        def _(d):
            hand_on(d).wait_send()

    @pl.loop(0, behind_next)
    def _(d):
        relay(d).wait_send()


def on_device(
    latents,
    clip_lengths,
    norm1_gain,
    conv1_weight,
    norm2_gain,
    conv2_weight,
    norm3_gain,
    query_weight,
    key_weight,
    value_weight,
    out_weight,
):
    frames, cells, width = latents.shape
    n = lax.axis_size("tm")
    reach = CLIP_MAX // frames
    lead = (CLIP_MAX // 2) // frames
    rows = frames * cells
    inner = HEADS * HEAD_DIM
    vmem = pl.BlockSpec(memory_space=pltpu.VMEM)
    smem = pl.BlockSpec(memory_space=pltpu.SMEM)
    hbm = pl.BlockSpec(memory_space=pl.ANY)
    dma = pltpu.SemaphoreType.DMA
    edge = pltpu.VMEM((2, cells, width), BF16)
    answer = pltpu.VMEM((HEADS, HEAD_DIM, rows), BF16)
    stats = pltpu.VMEM((2, HEADS, rows), F32)

    encoded = pl.pallas_call(
        functools.partial(block_kernel, n, reach, lead),
        out_shape=jax.ShapeDtypeStruct((rows, width), BF16),
        in_specs=[vmem, smem, vmem, vmem, vmem] + [hbm] * 6,
        out_specs=vmem,
        scratch_shapes=[
            pltpu.VMEM(conv1_weight.shape, BF16),
            pltpu.VMEM(conv2_weight.shape, BF16),
            pltpu.VMEM((width, inner), BF16),
            pltpu.VMEM((width, inner), BF16),
            pltpu.VMEM((width, inner), BF16),
            pltpu.VMEM((inner, width), BF16),
            pltpu.VMEM((frames + 2, cells + 2 * WT, 3 * width), BF16),
            edge,
            edge,
            edge,
            edge,
            pltpu.VMEM((rows, width), F32),
            pltpu.VMEM((rows, width), BF16),
            pltpu.VMEM((reach + reach // 2, rows, width), BF16),
            pltpu.VMEM((2, HEADS // 2, 256, 2 * rows), BF16),
            pltpu.VMEM((HEADS // 2, rows, 256), BF16),
            pltpu.VMEM((HEADS, VT_ROWS, rows), BF16),
            pltpu.VMEM((inner, width), BF16),
            pltpu.VMEM((inner, width), BF16),
            pltpu.VMEM((2, HEADS // 2, 8, 2 * rows), F32),
            pltpu.VMEM((2, HEADS, VT_ROWS, rows), F32),
            pltpu.VMEM((inner, rows), F32),
            answer,
            stats,
            answer,
            stats,
            dma((6,)),
            dma((2,)),
            dma((2,)),
            dma((reach + 1,)),
            dma((reach + 2,)),
            dma((reach // 2,)),
            dma((reach // 2,)),
            dma((reach // 2,)),
            dma,
            dma,
            dma((3,)),
            dma((3,)),
        ],
        compiler_params=pltpu.CompilerParams(
            collective_id=0, has_side_effects=True, vmem_limit_bytes=56 << 20
        ),
    )(
        latents,
        clip_lengths,
        norm1_gain.reshape(1, width),
        norm2_gain.reshape(1, width),
        norm3_gain.reshape(1, width),
        conv1_weight,
        conv2_weight,
        query_weight,
        key_weight,
        value_weight,
        out_weight,
    )
    return encoded.reshape(frames, cells, width)


def solution(mesh):
    return jax.shard_map(
        on_device,
        mesh=mesh,
        in_specs=(P(("groups", "tm"), None, None), P("groups")) + (P(),) * 9,
        out_specs=P(("groups", "tm"), None, None),
        check_vma=False,
    )
```
